32 devices in a mesh: blk: 8 (over z, x), mblk: 4 (over y, core).
Axes of the slice: x: 2, y: 2, z: 4, core: 2. Of those that a mesh axis runs over, the one named last changes fastest.
Arguments:
- alm: bfloat16 [3, 2, 2048, 8192], P(None, None, 'mblk', 'blk'), may hold values from -6 to 6
- legendre: bfloat16 [2048, 40, 8192], P('mblk', None, 'blk'), may hold values from -0.0625 to 0.0625
- m_value: int32 [2048], replicated, may hold values from 0 to 2047, each once
- cycle_weight: float32 [40], P('blk'), may hold values from 0.5 to 2
Outputs:
- bispec_alm: bfloat16 [2, 2048, 8192], P(None, 'mblk', 'blk')
The draws below stay inside these ranges and needn't reach their ends.
Inputs may be any that keep to these rules, and one draw needn't show every extreme that they name: m_value holds each order from 0 to 2047 exactly once.
All inputs are finite; a program needn't handle non-finite values.
Results may differ from the reference program's by a relative error of at most 0.0049.
Values may be sent and summed in bfloat16 or wider, within the bound.
No kernel may reach another device: no remote copies, remote signals or barrier semaphores. Data moves between devices by JAX's collectives and lax.ppermute only.
A program may use at most 128 MiB of HBM per device.

```python
import math
import jax
import jax.numpy as jnp
from jax import lax

M = 2048
L = 8192
NPHI = 32768
CYCLES = 40


def block_levels(key, extent, cuts, low, top_value):
    def one(dim, blocks):
        heights = jax.random.uniform(jax.random.fold_in(jax.random.fold_in(key, 6), dim), (blocks,), jnp.float32, low / len(cuts), top_value / len(cuts))
        return jnp.repeat(jnp.exp(heights), extent[dim] // blocks).reshape((-1,) + (1,) * (len(extent) - dim - 1))

    level = one(*cuts[0])
    for cut in cuts[1:]:
        level = level * one(*cut)
    return level


def centred(key, shape, spread, most, shards=(), kind=jnp.bfloat16):
    drawn = spread * jax.random.normal(key, shape, jnp.float32)
    if shards:
        drawn = drawn * block_levels(key, shape, shards, -0.22, 0.18)
    return jnp.clip(drawn, -most, most).astype(kind)


def setup_inputs(seed: int = 0) -> dict:
    arg_keys = jax.random.split(jax.random.key(seed), 5)
    return {
        "alm": centred(arg_keys[0], (3, 2, M, L), 1.0, 6.0, ((2, 4), (3, 8))),
        "legendre": centred(arg_keys[1], (M, CYCLES, L), L ** -0.5, 0.0625, ((0, 4), (2, 8))),
        "m_value": jax.random.permutation(arg_keys[2], M).astype(jnp.int32),
        "cycle_weight": jnp.clip(jnp.exp(math.log(2.0) - 1.3862944 * jax.random.uniform(arg_keys[3], (CYCLES,), jnp.float32) ** block_levels(arg_keys[3], (CYCLES,), ((0, 8),), -0.2, 0.2)), 0.5, 2.0),
    }


def reference(alm, legendre, m_value, cycle_weight):
    step_size = math.gcd(M, 128)
    block_count = M // step_size
    coeffs = alm.reshape(6, M, L)

    def synth_block(number):
        m_first = number * step_size
        leg_table = lax.dynamic_slice_in_dim(legendre, m_first, step_size, 0).astype(jnp.float32)
        coeff_part = lax.dynamic_slice_in_dim(coeffs, m_first, step_size, 1).astype(jnp.float32)
        return jnp.einsum('jml,mrl->rjm', coeff_part, leg_table, precision=lax.Precision.HIGHEST)
    blocks = lax.map(synth_block, jnp.arange(block_count, dtype=jnp.int32))
    spectra = jnp.moveaxis(blocks, 0, 2).reshape(CYCLES, 6, M)
    values = spectra.reshape(CYCLES, 3, 2, M)
    real_part = values[:, :, 0]
    imag_part = values[:, :, 1]
    real_full = jnp.zeros((CYCLES, 3, NPHI), real_part.dtype).at[:, :, m_value].set(real_part)
    imag_full = jnp.zeros((CYCLES, 3, NPHI), imag_part.dtype).at[:, :, m_value].set(imag_part)
    cycle_map = jnp.real(jnp.fft.ifft(lax.complex(real_full, imag_full), axis=-1)) * NPHI
    cycle_map = cycle_map * (1.0 / math.sqrt(M))
    product = cycle_map[:, 0] * cycle_map[:, 1] * cycle_map[:, 2]
    spectrum = jnp.fft.fft(product, axis=-1)[:, m_value]
    real_sum = jnp.real(spectrum)
    imag_sum = jnp.imag(spectrum)
    scale_rows = cycle_weight[:, None] * (1.0 / math.sqrt(NPHI))
    weighted = jnp.stack([real_sum * scale_rows, imag_sum * scale_rows], axis=1).astype(jnp.bfloat16)

    def analyse_block(number):
        m_first = number * step_size
        leg_table = lax.dynamic_slice_in_dim(legendre, m_first, step_size, 0).astype(jnp.float32)
        coeff_part = lax.dynamic_slice_in_dim(weighted, m_first, step_size, 2).astype(jnp.float32)
        return jnp.einsum('rjm,mrl->jml', coeff_part, leg_table, precision=lax.Precision.HIGHEST)
    blocks = lax.map(analyse_block, jnp.arange(block_count, dtype=jnp.int32))
    result = jnp.moveaxis(blocks, 0, 1).reshape(2, M, L)
    return (result * math.sqrt(L / CYCLES)).astype(jnp.bfloat16)
```

```python
import math

import jax
import jax.numpy as jnp
import numpy as np
from jax import lax
from jax.experimental import pallas as pl
from jax.experimental.pallas import tpu as pltpu
from jax.sharding import PartitionSpec as P

NPHI = 32768
LANES = 128

f32 = jnp.float32
bf16 = jnp.bfloat16


def grid_size(order_count):
    size = LANES
    while size <= 4 * (order_count - 1):
        size *= 2
    return min(size, NPHI)


def split_np(table):
    high = table.astype(jnp.bfloat16)
    low = (table - high.astype(np.float64)).astype(jnp.bfloat16)
    return high, low


def fourier_tables(order_count):
    size = grid_size(order_count)
    n2 = LANES
    n1 = size // n2
    k1 = order_count // n2
    turn = 2.0 * np.pi
    ang1 = turn * (np.outer(np.arange(n1), np.arange(k1)) % n1) / n1
    c1, s1 = np.cos(ang1), np.sin(ang1)
    ang2 = turn * (np.outer(np.arange(n2), np.arange(n2)) % n2) / n2
    c2, s2 = np.cos(ang2), np.sin(ang2)
    angt = turn * np.outer(np.arange(n1), np.arange(n2)) / size
    first = np.block([[c1, -s1], [s1, c1]])
    second = np.concatenate([c2, -s2], axis=0)
    third = np.concatenate([c2, -s2], axis=1)
    fourth = np.block([[c1.T, s1.T], [-s1.T, c1.T]])
    h, l = split_np(first)
    first3 = np.concatenate([h, h, l], axis=1)
    h, l = split_np(second)
    second3 = np.concatenate([h, h, l], axis=0)
    h, l = split_np(third)
    third3 = np.concatenate([h, h, l], axis=0)
    h, l = split_np(fourth)
    fourth3 = np.concatenate([h, h, l], axis=1)
    twiddle = np.stack([np.cos(angt), np.sin(angt)]).astype(np.float32)
    return first3, second3, third3, fourth3, twiddle


def split2(value):
    high = value.astype(bf16)
    low = (value - high.astype(f32)).astype(bf16)
    return high, low


def mm(a, b):
    return jnp.dot(a, b, preferred_element_type=f32)


def band_kernel(
    spec_ref, order_ref, own_ref, weight_ref, first_ref, second_ref, third_ref, fourth_ref, twid_ref,
    out_ref, high_ref, low_ref, *, cycles, order_count, copies,
):
    blocks, rows, width = spec_ref.shape
    n2 = LANES
    k1 = order_count // n2
    n1 = twid_ref.shape[1]
    orders = order_ref[...]
    mask1 = lax.broadcasted_iota(jnp.int32, (k1, order_count), 0) == orders // n2
    hot2 = (lax.broadcasted_iota(jnp.int32, (n2, order_count), 0) == orders % n2).astype(f32).astype(bf16)
    for row in range(rows):
        for block in range(blocks):
            lanes = slice(block * width, (block + 1) * width)
            value = spec_ref[block, row : row + 1, :]
            high = value.astype(bf16).astype(f32)
            low = value - high
            chosen = mask1[:, lanes]
            high_ref[row * k1 : (row + 1) * k1, lanes] = jnp.where(chosen, high, 0.0).astype(bf16)
            low_ref[row * k1 : (row + 1) * k1, lanes] = jnp.where(chosen, low, 0.0).astype(bf16)
    contract = (((1,), (1,)), ((), ()))
    ordered = lax.dot_general(high_ref[...], hot2, contract, preferred_element_type=f32)
    ordered = ordered + lax.dot_general(low_ref[...], hot2, contract, preferred_element_type=f32)
    first = first_ref[...]
    second = second_ref[...]
    third = third_ref[...]
    fourth = fourth_ref[...]
    cosine = twid_ref[0]
    sine = twid_ref[1]
    scale = 1.0 / math.sqrt(order_count)
    results = []
    for cycle in range(cycles):
        maps = None
        for field in range(3):
            start = (cycle * 3 + field) * 2 * k1
            high, low = split2(ordered[start : start + 2 * k1, :])
            part = mm(first, jnp.concatenate([high, low, high], axis=0))
            re, im = part[:n1], part[n1:]
            turned = jnp.concatenate([re * cosine - im * sine, re * sine + im * cosine], axis=1)
            high, low = split2(turned)
            cycle_map = mm(jnp.concatenate([high, low, high], axis=1), second) * scale
            maps = cycle_map if maps is None else maps * cycle_map
        high, low = split2(maps)
        part = mm(jnp.concatenate([high, low, high], axis=1), third)
        re, im = part[:, :n2], part[:, n2:]
        turned = jnp.concatenate([re * cosine + im * sine, im * cosine - re * sine], axis=0)
        high, low = split2(turned)
        sums = mm(fourth, jnp.concatenate([high, low, high], axis=0))
        results.append(sums * weight_ref[0, cycle])
    sums = jnp.concatenate(results, axis=0)
    high, low = split2(sums)
    own = own_ref[...]
    own_width = own.shape[1]
    own1 = lax.broadcasted_iota(jnp.int32, (k1, own_width), 0) == own // n2
    own2 = (lax.broadcasted_iota(jnp.int32, (n2, own_width), 0) == own % n2).astype(f32).astype(bf16)
    picked = mm(high, own2) + mm(low, own2)
    parts = []
    for row in range(2 * cycles):
        chosen = jnp.where(own1, picked[row * k1 : (row + 1) * k1, :], 0.0)
        parts.append(jnp.sum(chosen, axis=0, keepdims=True))
    weighted = jnp.concatenate(parts, axis=0).astype(bf16)
    for copy in range(copies):
        out_ref[copy] = weighted


def band_step(spectra, orders, own_orders, weights, cycles, copies):
    order_count = orders.shape[0]
    tables = fourier_tables(order_count)
    rows = spectra.shape[1]
    own = own_orders.shape[0]
    k1 = order_count // LANES
    vmem = pl.BlockSpec(memory_space=pltpu.VMEM)
    return pl.pallas_call(
        lambda *refs: band_kernel(*refs, cycles=cycles, order_count=order_count, copies=copies),
        out_shape=jax.ShapeDtypeStruct((copies, 2 * cycles, own), bf16),
        in_specs=[vmem, vmem, vmem, pl.BlockSpec(memory_space=pltpu.SMEM)] + [vmem] * 5,
        out_specs=vmem,
        scratch_shapes=[pltpu.VMEM((rows * k1, order_count), bf16)] * 2,
        compiler_params=pltpu.CompilerParams(vmem_limit_bytes=24 * 2**20),
        name="band",
    )(spectra, orders[None, :], own_orders[None, :], weights[None, :], *tables)


def shards(alm, legendre, m_value, cycle_weight):
    m_dev, cycle_count, l_dev = legendre.shape
    bands = lax.axis_size("blk")
    cycles = cycle_count // bands
    order_count = m_value.shape[0]
    coeffs = alm.reshape(6, m_dev, l_dev)
    own_orders = lax.dynamic_slice_in_dim(m_value, lax.axis_index("mblk") * m_dev, m_dev)
    partial_value = lax.dot_general(
        coeffs, legendre, (((2,), (2,)), ((1,), (0,))), preferred_element_type=f32
    )
    outgoing = jnp.transpose(partial_value, (2, 1, 0)).reshape(bands, cycles * 6, m_dev).astype(bf16)
    incoming = lax.all_to_all(outgoing, "blk", 0, 0, tiled=True)
    spectra = jnp.sum(incoming.astype(f32), axis=0)
    gathered = lax.all_gather(spectra, "mblk", axis=0)
    weights = cycle_weight * (NPHI / grid_size(order_count) / math.sqrt(NPHI))
    copies = band_step(gathered, m_value, own_orders, weights, cycles, bands)
    weighted = lax.all_to_all(copies, "blk", 0, 0, tiled=True)
    result = lax.dot_general(
        weighted.reshape(cycle_count, 2, m_dev),
        legendre,
        (((0,), (1,)), ((2,), (0,))),
        preferred_element_type=f32,
    )
    scale_factor = math.sqrt(l_dev * bands / cycle_count)
    return (jnp.transpose(result, (1, 0, 2)) * scale_factor).astype(bf16)


def solution(mesh):
    in_specs = (P(None, None, "mblk", "blk"), P("mblk", None, "blk"), P(), P("blk"))
    out_specs = P(None, "mblk", "blk")
    return jax.shard_map(shards, mesh=mesh, in_specs=in_specs, out_specs=out_specs, check_vma=False)
```

```python
import math

import jax
import jax.numpy as jnp
import numpy as np
from jax import lax
from jax.experimental import pallas as pl
from jax.experimental.pallas import tpu as pltpu
from jax.sharding import PartitionSpec as P

NPHI = 32768
LANES = 128

f32 = jnp.float32
bf16 = jnp.bfloat16


def grid_size(order_count):
    size = LANES
    while size <= 4 * (order_count - 1):
        size *= 2
    return min(size, NPHI)


def split_np(table):
    high = table.astype(jnp.bfloat16)
    low = (table - high.astype(np.float64)).astype(jnp.bfloat16)
    return high, low


def fourier_tables(order_count):
    size = grid_size(order_count)
    n2 = LANES
    n1 = size // n2
    k1 = order_count // n2
    turn = 2.0 * np.pi
    ang1 = turn * (np.outer(np.arange(n1), np.arange(k1)) % n1) / n1
    c1, s1 = np.cos(ang1), np.sin(ang1)
    ang2 = turn * (np.outer(np.arange(n2), np.arange(n2)) % n2) / n2
    c2, s2 = np.cos(ang2), np.sin(ang2)
    angt = turn * np.outer(np.arange(n1), np.arange(n2)) / size
    first = np.block([[c1, -s1], [s1, c1]])
    second = np.concatenate([c2, -s2], axis=0)
    third = np.concatenate([c2, -s2], axis=1)
    fourth = np.block([[c1.T, s1.T], [-s1.T, c1.T]])
    h, l = split_np(first)
    first3 = np.concatenate([h, h, l], axis=1)
    h, l = split_np(second)
    second3 = np.concatenate([h, h, l], axis=0)
    h, l = split_np(third)
    third3 = np.concatenate([h, h, l], axis=0)
    h, l = split_np(fourth)
    fourth3 = np.concatenate([h, h, l], axis=1)
    twiddle = np.stack([np.cos(angt), np.sin(angt)]).astype(np.float32)
    return first3, second3, third3, fourth3, twiddle


def split2(value):
    high = value.astype(bf16)
    low = (value - high.astype(f32)).astype(bf16)
    return high, low


def mm(a, b):
    return jnp.dot(a, b, preferred_element_type=f32)


def band_kernel(
    place_ref, spec_ref, order_ref, weight_ref, first_ref, second_ref, third_ref, fourth_ref, twid_ref,
    out_ref, high_ref, low_ref, line_ref, *, order_count, copies,
):
    blocks, rows, width = spec_ref.shape
    cycles = rows // 6
    n2 = LANES
    k1 = order_count // n2
    n1 = twid_ref.shape[1]
    orders = order_ref[...]
    mask1 = lax.broadcasted_iota(jnp.int32, (k1, order_count), 0) == orders // n2
    mask1 = jnp.where(mask1, 1.0, 0.0).astype(bf16)
    hot2 = lax.broadcasted_iota(jnp.int32, (n2, order_count), 0) == orders % n2
    hot2 = jnp.where(hot2, 1.0, 0.0).astype(bf16)
    for block in range(blocks):
        lanes = slice(block * width, (block + 1) * width)
        value = spec_ref[block]
        low = value - value.astype(bf16).astype(f32)
        line_ref[...] = low
        for row in range(rows):
            span = slice(row * k1, (row + 1) * k1)
            high_ref[span, lanes] = (
                jnp.broadcast_to(spec_ref[block, row : row + 1, :], (k1, width)).astype(bf16) * mask1[:, lanes]
            )
            low_ref[span, lanes] = (
                jnp.broadcast_to(line_ref[row : row + 1, :], (k1, width)).astype(bf16) * mask1[:, lanes]
            )
    contract = (((1,), (1,)), ((), ()))
    ordered = lax.dot_general(high_ref[...], hot2, contract, preferred_element_type=f32)
    ordered = ordered + lax.dot_general(low_ref[...], hot2, contract, preferred_element_type=f32)
    cosine = twid_ref[0]
    sine = twid_ref[1]
    scale = 1.0 / math.sqrt(order_count)
    columns = []
    for cycle in range(cycles):
        for field in range(3):
            first_row = (2 * field * cycles + cycle) * k1
            second_row = first_row + cycles * k1
            columns.append(
                jnp.concatenate(
                    [ordered[first_row : first_row + k1, :], ordered[second_row : second_row + k1, :]], axis=0
                )
            )
    high, low = split2(jnp.concatenate(columns, axis=1))
    part = mm(first_ref[...], jnp.concatenate([high, low, high], axis=0))
    turned = []
    for column in range(3 * cycles):
        lanes = slice(column * n2, (column + 1) * n2)
        re, im = part[:n1, lanes], part[n1:, lanes]
        turned.append(jnp.concatenate([re * cosine - im * sine, re * sine + im * cosine], axis=1))
    high, low = split2(jnp.concatenate(turned, axis=0))
    maps = mm(jnp.concatenate([high, low, high], axis=1), second_ref[...]) * scale
    products = []
    for cycle in range(cycles):
        start = 3 * cycle * n1
        product = maps[start : start + n1] * maps[start + n1 : start + 2 * n1]
        products.append(product * maps[start + 2 * n1 : start + 3 * n1])
    high, low = split2(jnp.concatenate(products, axis=0))
    part = mm(jnp.concatenate([high, low, high], axis=1), third_ref[...])
    turned = []
    for cycle in range(cycles):
        re, im = part[cycle * n1 : (cycle + 1) * n1, :n2], part[cycle * n1 : (cycle + 1) * n1, n2:]
        turned.append(jnp.concatenate([re * cosine + im * sine, im * cosine - re * sine], axis=0))
    high, low = split2(jnp.concatenate(turned, axis=1))
    sums = mm(fourth_ref[...], jnp.concatenate([high, low, high], axis=0))
    factor = NPHI / (n1 * n2) / math.sqrt(NPHI)
    results = [
        sums[:, cycle * n2 : (cycle + 1) * n2] * (weight_ref[0, cycle] * factor) for cycle in range(cycles)
    ]
    high, low = split2(jnp.concatenate(results, axis=0))
    own = order_ref[:, pl.ds(place_ref[0] * width, width)]
    own1 = lax.broadcasted_iota(jnp.int32, (k1, width), 0) == own // n2
    own2 = lax.broadcasted_iota(jnp.int32, (n2, width), 0) == own % n2
    own2 = jnp.where(own2, 1.0, 0.0).astype(bf16)
    picked = mm(jnp.concatenate([high, low], axis=1), jnp.concatenate([own2, own2], axis=0))
    parts = []
    for part in range(2):
        for cycle in range(cycles):
            row = (2 * cycle + part) * k1
            chosen = jnp.where(own1, picked[row : row + k1, :], 0.0)
            parts.append(jnp.sum(chosen, axis=0, keepdims=True))
    weighted = jnp.concatenate(parts, axis=0).astype(bf16)
    for copy in range(copies):
        out_ref[copy] = weighted


def band_step(place, spectra, orders, weights, copies):
    order_count = orders.shape[0]
    tables = fourier_tables(order_count)
    blocks, rows, width = spectra.shape
    k1 = order_count // LANES
    smem = pl.BlockSpec(memory_space=pltpu.SMEM)
    vmem = pl.BlockSpec(memory_space=pltpu.VMEM)
    return pl.pallas_call(
        lambda *refs: band_kernel(*refs, order_count=order_count, copies=copies),
        out_shape=pltpu.VMEM((copies, rows // 3, width), bf16),
        in_specs=[smem, vmem, vmem, smem] + [vmem] * 5,
        out_specs=vmem,
        scratch_shapes=[pltpu.VMEM((rows * k1, order_count), bf16)] * 2 + [pltpu.VMEM((rows, width), f32)],
        compiler_params=pltpu.CompilerParams(vmem_limit_bytes=12 * 2**20),
        name="band",
    )(place, spectra, orders[None, :], weights[None, :], *tables)


CHUNK = 32
GROUP = 16
STEP = 32
AHEAD = 3


def synthesis_kernel(alm_ref, leg_ref, out_ref, keep_ref, alm_buf, acc_ref, row_ref, alm_sem, leg_sem, *, bands):
    fields, m_dev, l_dev = alm_ref.shape
    cycle_count = leg_ref.shape[1]
    cycles = cycle_count // bands
    chunks = m_dev // STEP
    per_tile = LANES // GROUP

    def alm_copy(chunk):
        rows = pl.ds(chunk * STEP, STEP)
        return pltpu.make_async_copy(alm_ref.at[:, rows], alm_buf.at[:, rows], alm_sem.at[chunk])

    def leg_copy(chunk):
        rows = pl.ds(chunk * STEP, STEP)
        return pltpu.make_async_copy(leg_ref.at[rows], keep_ref.at[rows], leg_sem.at[chunk])

    for chunk in range(min(AHEAD, chunks)):
        alm_copy(chunk).start()
        leg_copy(chunk).start()
    width = fields * GROUP
    lane = lax.broadcasted_iota(jnp.int32, (1, width), 1) % GROUP
    tile_lane = lax.broadcasted_iota(jnp.int32, (1, LANES), 1) // GROUP

    def one_tile(tile, carry):
        sums = [None] * fields
        for place in range(per_tile):
            number = tile * per_tile + place
            if place * GROUP % STEP == 0:
                chunk = number * GROUP // STEP

                @pl.when(chunk + AHEAD < chunks)
                def _():
                    alm_copy(chunk + AHEAD).start()
                    leg_copy(chunk + AHEAD).start()

                alm_copy(chunk).wait()
                leg_copy(chunk).wait()
            rows = pl.ds(number * GROUP, GROUP)
            right = alm_buf[:, rows, :].reshape(width, l_dev)
            own = None
            for half in range(2):
                left = keep_ref[pl.ds(number * GROUP + half * GROUP // 2, GROUP // 2)]
                both = lax.dot_general(
                    left.reshape(GROUP // 2 * cycle_count, l_dev),
                    right,
                    (((1,), (1,)), ((), ())),
                    preferred_element_type=f32,
                )
                for order in range(GROUP // 2):
                    part = both[order * cycle_count : (order + 1) * cycle_count]
                    part = jnp.where(lane == half * GROUP // 2 + order, part, 0.0)
                    own = part if own is None else own + part
            own = jnp.concatenate([own, jnp.zeros((cycle_count, LANES - width), f32)], axis=1)
            for field in range(fields):
                shift = (place - field) * GROUP % LANES
                moved = pltpu.roll(own, shift, 1) if shift else own
                moved = jnp.where(tile_lane == place, moved, 0.0)
                sums[field] = moved if sums[field] is None else sums[field] + moved
        for field in range(fields):
            acc_ref[tile, field] = sums[field]
        return carry

    lax.fori_loop(0, m_dev // LANES, one_tile, 0)
    for tile in range(m_dev // LANES):
        lanes = slice(tile * LANES, (tile + 1) * LANES)
        for band in range(bands):
            for field in range(fields):
                row_ref[band, field * cycles : (field + 1) * cycles, lanes] = acc_ref[
                    tile, field, band * cycles : (band + 1) * cycles, :
                ]
    out_ref[...] = row_ref[...].astype(bf16)


def synthesis(coeffs, legendre, bands):
    fields, m_dev, l_dev = coeffs.shape
    cycle_count = legendre.shape[1]
    rows = fields * cycle_count // bands
    chunks = m_dev // STEP
    hbm = pl.BlockSpec(memory_space=pl.ANY)
    vmem = pl.BlockSpec(memory_space=pltpu.VMEM)
    return pl.pallas_call(
        lambda *refs: synthesis_kernel(*refs, bands=bands),
        out_shape=[
            jax.ShapeDtypeStruct((bands, rows, m_dev), bf16),
            pltpu.VMEM(legendre.shape, bf16),
        ],
        in_specs=[hbm, hbm],
        out_specs=[vmem, vmem],
        scratch_shapes=[
            pltpu.VMEM(coeffs.shape, bf16),
            pltpu.VMEM((m_dev // LANES, fields, cycle_count, LANES), f32),
            pltpu.VMEM((bands, rows, m_dev), f32),
            pltpu.SemaphoreType.DMA((chunks,)),
            pltpu.SemaphoreType.DMA((chunks,)),
        ],
        compiler_params=pltpu.CompilerParams(vmem_limit_bytes=14 * 2**20),
        name="synthesis",
    )(
        pltpu.with_memory_space_constraint(coeffs, pltpu.HBM),
        pltpu.with_memory_space_constraint(legendre, pltpu.HBM),
    )


def analysis_kernel(weighted_ref, keep_ref, out_ref, rows_ref, wide_ref, buf_ref, sem, *, scale):
    bands, part_rows, m_dev = weighted_ref.shape
    cycles = part_rows // 2
    cycle_count, l_dev = keep_ref.shape[1:]
    width = CHUNK * cycle_count
    spread = lax.broadcasted_iota(jnp.int32, (cycle_count, width), 1) % cycle_count
    spread = (spread == lax.broadcasted_iota(jnp.int32, (cycle_count, width), 0)).astype(f32).astype(bf16)
    for part in range(2):
        for band in range(bands):
            rows_ref[part, band * cycles : (band + 1) * cycles, :] = weighted_ref[
                band, part * cycles : (part + 1) * cycles, :
            ].astype(f32)
        wide_ref[part] = rows_ref[part].T.astype(bf16)
    diagonal = lax.broadcasted_iota(jnp.int32, (CHUNK, width), 1) // cycle_count
    diagonal = diagonal == lax.broadcasted_iota(jnp.int32, (CHUNK, width), 0)

    def out_copy(chunk, slot):
        return pltpu.make_async_copy(
            buf_ref.at[slot], out_ref.at[:, pl.ds(chunk * CHUNK, CHUNK)], sem.at[slot]
        )

    def one_chunk(chunk, carry):
        slot = chunk % 2
        rows = pl.ds(chunk * CHUNK, CHUNK)
        parts = [
            jnp.where(diagonal, mm(wide_ref[part, rows, :], spread), 0.0).astype(bf16) for part in range(2)
        ]
        left = jnp.concatenate(parts, axis=0)
        right = keep_ref[rows].reshape(width, l_dev)
        result = mm(left, right) * scale

        @pl.when(chunk >= 2)
        def _():
            out_copy(chunk - 2, slot).wait()

        buf_ref[slot] = result.reshape(2, CHUNK, l_dev).astype(bf16)
        out_copy(chunk, slot).start()
        return carry

    chunks = m_dev // CHUNK
    lax.fori_loop(0, chunks, one_chunk, 0)
    for chunk in range(max(chunks - 2, 0), chunks):
        out_copy(chunk, chunk % 2).wait()


def analysis(weighted, keep, scale):
    m_dev, cycle_count, l_dev = keep.shape
    vmem = pl.BlockSpec(memory_space=pltpu.VMEM)
    return pl.pallas_call(
        lambda *refs: analysis_kernel(*refs, scale=scale),
        out_shape=jax.ShapeDtypeStruct((2, m_dev, l_dev), bf16),
        in_specs=[vmem, vmem],
        out_specs=pl.BlockSpec(memory_space=pl.ANY),
        scratch_shapes=[
            pltpu.VMEM((2, cycle_count, m_dev), f32),
            pltpu.VMEM((2, m_dev, cycle_count), bf16),
            pltpu.VMEM((2, 2, CHUNK, l_dev), bf16),
            pltpu.SemaphoreType.DMA((2,)),
        ],
        compiler_params=pltpu.CompilerParams(vmem_limit_bytes=14 * 2**20),
        name="analysis",
    )(
        pltpu.with_memory_space_constraint(weighted, pltpu.VMEM),
        pltpu.with_memory_space_constraint(keep, pltpu.VMEM),
    )


def shards(alm, legendre, m_value, cycle_weight):
    m_dev, cycle_count, l_dev = legendre.shape
    bands = lax.axis_size("blk")
    place = lax.axis_index("mblk").astype(jnp.int32)[None]
    outgoing, keep = synthesis(alm.reshape(6, m_dev, l_dev), legendre, bands)
    outgoing, place, cycle_weight = lax.optimization_barrier((outgoing, place, cycle_weight))
    incoming = lax.all_to_all(outgoing, "blk", 0, 0, tiled=True)
    spectra = jnp.sum(incoming.astype(f32), axis=0)
    gathered = lax.all_gather(spectra, "mblk", axis=0)
    copies = band_step(place, gathered, m_value, cycle_weight, bands)
    weighted = lax.all_to_all(copies, "blk", 0, 0, tiled=True)
    return analysis(weighted, keep, math.sqrt(l_dev * bands / cycle_count))


def solution(mesh):
    in_specs = (P(None, None, "mblk", "blk"), P("mblk", None, "blk"), P(), P("blk"))
    out_specs = P(None, "mblk", "blk")
    return jax.shard_map(shards, mesh=mesh, in_specs=in_specs, out_specs=out_specs, check_vma=False)
```

```python
import math

import jax
import jax.numpy as jnp
import numpy as np
from jax import lax
from jax.experimental import pallas as pl
from jax.experimental.pallas import tpu as pltpu
from jax.sharding import PartitionSpec as P

NPHI = 32768
LANES = 128

f32 = jnp.float32
bf16 = jnp.bfloat16


def grid_size(order_count):
    size = LANES
    while size <= 4 * (order_count - 1):
        size *= 2
    return min(size, NPHI)


def split_np(table):
    high = table.astype(jnp.bfloat16)
    low = (table - high.astype(np.float64)).astype(jnp.bfloat16)
    return high, low


def fourier_tables(order_count):
    size = grid_size(order_count)
    n2 = LANES
    n1 = size // n2
    k1 = order_count // n2
    turn = 2.0 * np.pi
    ang1 = turn * (np.outer(np.arange(n1), np.arange(k1)) % n1) / n1
    c1, s1 = np.cos(ang1), np.sin(ang1)
    ang2 = turn * (np.outer(np.arange(n2), np.arange(n2)) % n2) / n2
    c2, s2 = np.cos(ang2), np.sin(ang2)
    angt = turn * np.outer(np.arange(n1), np.arange(n2)) / size
    first = np.block([[c1, -s1], [s1, c1]])
    second = np.concatenate([c2, -s2], axis=0)
    third = np.concatenate([c2, -s2], axis=1)
    fourth = np.block([[c1.T, s1.T], [-s1.T, c1.T]])
    h, l = split_np(first)
    first3 = np.concatenate([h, h, l], axis=1)
    h, l = split_np(second)
    second3 = np.concatenate([h, h, l], axis=0)
    h, l = split_np(third)
    third3 = np.concatenate([h, h, l], axis=0)
    h, l = split_np(fourth)
    fourth3 = np.concatenate([h, h, l], axis=1)
    twiddle = np.stack([np.cos(angt), np.sin(angt)]).astype(np.float32)
    return first3, second3, third3, fourth3, twiddle


def split2(value):
    high = value.astype(bf16)
    low = (value - high.astype(f32)).astype(bf16)
    return high, low


def mm(a, b):
    return jnp.dot(a, b, preferred_element_type=f32)


def mm_pieces(a, b):
    total = None
    for first in range(0, a.shape[1], LANES):
        part = mm(a[:, first : first + LANES], b[first : first + LANES])
        total = part if total is None else total + part
    return total


def band_kernel(
    place_ref, spec_ref, order_ref, weight_ref, first_ref, second_ref, third_ref, fourth_ref, twid_ref,
    out_ref, high_ref, low_ref, line_ref, *, order_count, copies,
):
    blocks, rows, width = spec_ref.shape
    cycles = rows // 6
    n2 = LANES
    k1 = order_count // n2
    n1 = twid_ref.shape[1]
    orders = order_ref[...]
    mask1 = lax.broadcasted_iota(jnp.int32, (k1, order_count), 0) == orders // n2
    mask1 = jnp.where(mask1, 1.0, 0.0).astype(bf16)
    hot2 = lax.broadcasted_iota(jnp.int32, (n2, order_count), 0) == orders % n2
    hot2 = jnp.where(hot2, 1.0, 0.0).astype(bf16)
    for block in range(blocks):
        lanes = slice(block * width, (block + 1) * width)
        value = spec_ref[block]
        low = value - value.astype(bf16).astype(f32)
        line_ref[...] = low
        for row in range(rows):
            span = slice(row * k1, (row + 1) * k1)
            high_ref[span, lanes] = (
                jnp.broadcast_to(spec_ref[block, row : row + 1, :], (k1, width)).astype(bf16) * mask1[:, lanes]
            )
            low_ref[span, lanes] = (
                jnp.broadcast_to(line_ref[row : row + 1, :], (k1, width)).astype(bf16) * mask1[:, lanes]
            )
    contract = (((1,), (1,)), ((), ()))
    ordered = lax.dot_general(high_ref[...], hot2, contract, preferred_element_type=f32)
    ordered = ordered + lax.dot_general(low_ref[...], hot2, contract, preferred_element_type=f32)
    cosine = twid_ref[0]
    sine = twid_ref[1]
    scale = 1.0 / math.sqrt(order_count)
    columns = []
    for cycle in range(cycles):
        for field in range(3):
            first_row = (2 * field * cycles + cycle) * k1
            second_row = first_row + cycles * k1
            columns.append(
                jnp.concatenate(
                    [ordered[first_row : first_row + k1, :], ordered[second_row : second_row + k1, :]], axis=0
                )
            )
    high, low = split2(jnp.concatenate(columns, axis=1))
    part = mm(first_ref[...], jnp.concatenate([high, low, high], axis=0))
    turned = []
    for column in range(3 * cycles):
        lanes = slice(column * n2, (column + 1) * n2)
        re, im = part[:n1, lanes], part[n1:, lanes]
        turned.append(jnp.concatenate([re * cosine - im * sine, re * sine + im * cosine], axis=1))
    high, low = split2(jnp.concatenate(turned, axis=0))
    maps = mm(jnp.concatenate([high, low, high], axis=1), second_ref[...]) * scale
    products = []
    for cycle in range(cycles):
        start = 3 * cycle * n1
        product = maps[start : start + n1] * maps[start + n1 : start + 2 * n1]
        products.append(product * maps[start + 2 * n1 : start + 3 * n1])
    high, low = split2(jnp.concatenate(products, axis=0))
    part = mm(jnp.concatenate([high, low, high], axis=1), third_ref[...])
    turned = []
    for cycle in range(cycles):
        re, im = part[cycle * n1 : (cycle + 1) * n1, :n2], part[cycle * n1 : (cycle + 1) * n1, n2:]
        turned.append(jnp.concatenate([re * cosine + im * sine, im * cosine - re * sine], axis=0))
    high, low = split2(jnp.concatenate(turned, axis=1))
    sums = mm(fourth_ref[...], jnp.concatenate([high, low, high], axis=0))
    factor = NPHI / (n1 * n2) / math.sqrt(NPHI)
    results = [
        sums[:, cycle * n2 : (cycle + 1) * n2] * (weight_ref[0, cycle] * factor) for cycle in range(cycles)
    ]
    high, low = split2(jnp.concatenate(results, axis=0))
    own = order_ref[:, pl.ds(place_ref[0] * width, width)]
    own1 = lax.broadcasted_iota(jnp.int32, (k1, width), 0) == own // n2
    own2 = lax.broadcasted_iota(jnp.int32, (n2, width), 0) == own % n2
    own2 = jnp.where(own2, 1.0, 0.0).astype(bf16)
    picked = mm(jnp.concatenate([high, low], axis=1), jnp.concatenate([own2, own2], axis=0))
    parts = []
    for part in range(2):
        for cycle in range(cycles):
            row = (2 * cycle + part) * k1
            chosen = jnp.where(own1, picked[row : row + k1, :], 0.0)
            parts.append(jnp.sum(chosen, axis=0, keepdims=True))
    weighted = jnp.concatenate(parts, axis=0).astype(bf16)
    for copy in range(copies):
        out_ref[copy] = weighted


def band_step(place, spectra, orders, weights, copies):
    order_count = orders.shape[0]
    tables = fourier_tables(order_count)
    blocks, rows, width = spectra.shape
    k1 = order_count // LANES
    smem = pl.BlockSpec(memory_space=pltpu.SMEM)
    vmem = pl.BlockSpec(memory_space=pltpu.VMEM)
    return pl.pallas_call(
        lambda *refs: band_kernel(*refs, order_count=order_count, copies=copies),
        out_shape=pltpu.VMEM((copies, rows // 3, width), bf16),
        in_specs=[smem, vmem, vmem, smem] + [vmem] * 5,
        out_specs=vmem,
        scratch_shapes=[pltpu.VMEM((rows * k1, order_count), bf16)] * 2 + [pltpu.VMEM((rows, width), f32)],
        compiler_params=pltpu.CompilerParams(vmem_limit_bytes=12 * 2**20),
        name="band",
    )(place, spectra, orders[None, :], weights[None, :], *tables)


CHUNK = 32
GROUP = 16
PAIR = 4
STEP = 32
AHEAD = 3


def synthesis_kernel(alm_ref, leg_ref, out_ref, keep_ref, alm_buf, acc_ref, row_ref, alm_sem, leg_sem, *, bands):
    fields, m_dev, l_dev = alm_ref.shape
    cycle_count = leg_ref.shape[1]
    cycles = cycle_count // bands
    chunks = m_dev // STEP
    per_tile = LANES // GROUP

    def alm_copy(chunk):
        rows = pl.ds(chunk * STEP, STEP)
        return pltpu.make_async_copy(alm_ref.at[:, rows], alm_buf.at[:, rows], alm_sem.at[chunk])

    def leg_copy(chunk):
        rows = pl.ds(chunk * STEP, STEP)
        return pltpu.make_async_copy(leg_ref.at[rows], keep_ref.at[rows], leg_sem.at[chunk])

    for chunk in range(min(AHEAD, chunks)):
        alm_copy(chunk).start()
        leg_copy(chunk).start()
    width = fields * GROUP
    lane = lax.broadcasted_iota(jnp.int32, (1, width), 1) % GROUP
    tile_lane = lax.broadcasted_iota(jnp.int32, (1, LANES), 1) // GROUP

    def one_tile(tile, carry):
        sums = [None] * fields
        for place in range(per_tile):
            number = tile * per_tile + place
            if place * GROUP % STEP == 0:
                chunk = number * GROUP // STEP

                @pl.when(chunk + AHEAD < chunks)
                def _():
                    alm_copy(chunk + AHEAD).start()
                    leg_copy(chunk + AHEAD).start()

                alm_copy(chunk).wait()
                leg_copy(chunk).wait()
            rows = pl.ds(number * GROUP, GROUP)
            right = alm_buf[:, rows, :].reshape(width, l_dev)
            own = None
            for half in range(2):
                left = keep_ref[pl.ds(number * GROUP + half * GROUP // 2, GROUP // 2)]
                both = lax.dot_general(
                    left.reshape(GROUP // 2 * cycle_count, l_dev),
                    right,
                    (((1,), (1,)), ((), ())),
                    preferred_element_type=f32,
                )
                for order in range(GROUP // 2):
                    part = both[order * cycle_count : (order + 1) * cycle_count]
                    part = jnp.where(lane == half * GROUP // 2 + order, part, 0.0)
                    own = part if own is None else own + part
            own = jnp.concatenate([own, jnp.zeros((cycle_count, LANES - width), f32)], axis=1)
            for field in range(fields):
                shift = (place - field) * GROUP % LANES
                moved = pltpu.roll(own, shift, 1) if shift else own
                moved = jnp.where(tile_lane == place, moved, 0.0)
                sums[field] = moved if sums[field] is None else sums[field] + moved
        for field in range(fields):
            acc_ref[tile, field] = sums[field]
        return carry

    lax.fori_loop(0, m_dev // LANES, one_tile, 0)
    for tile in range(m_dev // LANES):
        lanes = slice(tile * LANES, (tile + 1) * LANES)
        for band in range(bands):
            for field in range(fields):
                row_ref[band, field * cycles : (field + 1) * cycles, lanes] = acc_ref[
                    tile, field, band * cycles : (band + 1) * cycles, :
                ]
    out_ref[...] = row_ref[...].astype(bf16)


def synthesis(coeffs, legendre, bands):
    fields, m_dev, l_dev = coeffs.shape
    cycle_count = legendre.shape[1]
    rows = fields * cycle_count // bands
    chunks = m_dev // STEP
    hbm = pl.BlockSpec(memory_space=pl.ANY)
    vmem = pl.BlockSpec(memory_space=pltpu.VMEM)
    return pl.pallas_call(
        lambda *refs: synthesis_kernel(*refs, bands=bands),
        out_shape=[
            jax.ShapeDtypeStruct((bands, rows, m_dev), bf16),
            pltpu.VMEM(legendre.shape, bf16),
        ],
        in_specs=[hbm, hbm],
        out_specs=[vmem, vmem],
        scratch_shapes=[
            pltpu.VMEM(coeffs.shape, bf16),
            pltpu.VMEM((m_dev // LANES, fields, cycle_count, LANES), f32),
            pltpu.VMEM((bands, rows, m_dev), f32),
            pltpu.SemaphoreType.DMA((chunks,)),
            pltpu.SemaphoreType.DMA((chunks,)),
        ],
        compiler_params=pltpu.CompilerParams(vmem_limit_bytes=14 * 2**20),
        name="synthesis",
    )(
        pltpu.with_memory_space_constraint(coeffs, pltpu.HBM),
        pltpu.with_memory_space_constraint(legendre, pltpu.HBM),
    )


def analysis_kernel(weighted_ref, keep_ref, out_ref, rows_ref, wide_ref, left_ref, buf_ref, sem, *, scale):
    bands, part_rows, m_dev = weighted_ref.shape
    cycles = part_rows // 2
    cycle_count, l_dev = keep_ref.shape[1:]
    width = CHUNK * cycle_count
    pair = left_ref.shape[1]
    chunks = m_dev // CHUNK
    steps = chunks // pair
    spread = lax.broadcasted_iota(jnp.int32, (cycle_count, width), 1) % cycle_count
    spread = spread == lax.broadcasted_iota(jnp.int32, (cycle_count, width), 0)
    spread = jnp.where(spread, 1.0, 0.0).astype(bf16)
    for part in range(2):
        for band in range(bands):
            rows_ref[part, band * cycles : (band + 1) * cycles, :] = weighted_ref[
                band, part * cycles : (part + 1) * cycles, :
            ].astype(f32)
        wide_ref[:, part] = rows_ref[part].T.astype(bf16).reshape(chunks, CHUNK, cycle_count)
    diagonal = lax.broadcasted_iota(jnp.int32, (CHUNK, width), 1) // cycle_count
    diagonal = diagonal == lax.broadcasted_iota(jnp.int32, (CHUNK, width), 0)

    def build(step, slot):
        source = wide_ref[pl.ds(step * pair, pair)].reshape(pair * 2 * CHUNK, cycle_count)
        tiled = mm(source, spread).reshape(pair, 2, CHUNK, width)
        chosen = jnp.where(diagonal, tiled, 0.0).astype(bf16)
        left_ref[slot] = chosen.reshape(pair, 2 * CHUNK, width)

    def out_copy(step, slot):
        rows = pl.ds(step * pair * CHUNK, pair * CHUNK)
        return pltpu.make_async_copy(buf_ref.at[slot], out_ref.at[:, rows], sem.at[slot])

    build(0, 0)

    def one_step(step, carry):
        slot = step % 2

        @pl.when(step >= 2)
        def _():
            out_copy(step - 2, slot).wait()

        for item in range(pair):
            rows = pl.ds((step * pair + item) * CHUNK, CHUNK)
            right = keep_ref[rows].reshape(width, l_dev)
            result = mm_pieces(left_ref[slot, item], right) * scale
            buf_ref[slot, :, item * CHUNK : (item + 1) * CHUNK, :] = result.reshape(2, CHUNK, l_dev).astype(bf16)
        build(jnp.minimum(step + 1, steps - 1), 1 - slot)
        out_copy(step, slot).start()
        return carry

    lax.fori_loop(0, steps, one_step, 0)
    for step in range(max(steps - 2, 0), steps):
        out_copy(step, step % 2).wait()


def analysis(weighted, keep, scale):
    m_dev, cycle_count, l_dev = keep.shape
    vmem = pl.BlockSpec(memory_space=pltpu.VMEM)
    chunks = m_dev // CHUNK
    pair = math.gcd(chunks, PAIR)
    return pl.pallas_call(
        lambda *refs: analysis_kernel(*refs, scale=scale),
        out_shape=jax.ShapeDtypeStruct((2, m_dev, l_dev), bf16),
        in_specs=[vmem, vmem],
        out_specs=pl.BlockSpec(memory_space=pl.ANY),
        scratch_shapes=[
            pltpu.VMEM((2, cycle_count, m_dev), f32),
            pltpu.VMEM((chunks, 2, CHUNK, cycle_count), bf16),
            pltpu.VMEM((2, pair, 2 * CHUNK, CHUNK * cycle_count), bf16),
            pltpu.VMEM((2, 2, pair * CHUNK, l_dev), bf16),
            pltpu.SemaphoreType.DMA((2,)),
        ],
        compiler_params=pltpu.CompilerParams(vmem_limit_bytes=14 * 2**20),
        name="analysis",
    )(
        pltpu.with_memory_space_constraint(weighted, pltpu.VMEM),
        pltpu.with_memory_space_constraint(keep, pltpu.VMEM),
    )


def shards(alm, legendre, m_value, cycle_weight):
    m_dev, cycle_count, l_dev = legendre.shape
    bands = lax.axis_size("blk")
    place = lax.axis_index("mblk").astype(jnp.int32)[None]
    outgoing, keep = synthesis(alm.reshape(6, m_dev, l_dev), legendre, bands)
    outgoing, place, cycle_weight = lax.optimization_barrier((outgoing, place, cycle_weight))
    incoming = lax.all_to_all(outgoing, "blk", 0, 0, tiled=True)
    spectra = jnp.sum(incoming.astype(f32), axis=0)
    gathered = lax.all_gather(spectra, "mblk", axis=0)
    copies = band_step(place, gathered, m_value, cycle_weight, bands)
    weighted = lax.all_to_all(copies, "blk", 0, 0, tiled=True)
    return analysis(weighted, keep, math.sqrt(l_dev * bands / cycle_count))


def solution(mesh):
    in_specs = (P(None, None, "mblk", "blk"), P("mblk", None, "blk"), P(), P("blk"))
    out_specs = P(None, "mblk", "blk")
    return jax.shard_map(shards, mesh=mesh, in_specs=in_specs, out_specs=out_specs, check_vma=False)
```

```python
import math

import jax
import jax.numpy as jnp
import numpy as np
from jax import lax
from jax.experimental import pallas as pl
from jax.experimental.pallas import tpu as pltpu
from jax.sharding import PartitionSpec as P

NPHI = 32768
LANES = 128

f32 = jnp.float32
bf16 = jnp.bfloat16


def grid_size(order_count):
    size = LANES
    while size <= 4 * (order_count - 1):
        size *= 2
    return min(size, NPHI)


def split_np(table):
    high = table.astype(jnp.bfloat16)
    low = (table - high.astype(np.float64)).astype(jnp.bfloat16)
    return high, low


def fourier_tables(order_count):
    size = grid_size(order_count)
    n2 = LANES
    n1 = size // n2
    k1 = order_count // n2
    turn = 2.0 * np.pi
    ang1 = turn * (np.outer(np.arange(n1), np.arange(k1)) % n1) / n1
    c1, s1 = np.cos(ang1), np.sin(ang1)
    ang2 = turn * (np.outer(np.arange(n2), np.arange(n2)) % n2) / n2
    c2, s2 = np.cos(ang2), np.sin(ang2)
    angt = turn * np.outer(np.arange(n1), np.arange(n2)) / size
    first = np.block([[c1, -s1], [s1, c1]])
    second = np.concatenate([c2, -s2], axis=0)
    third = np.concatenate([c2, -s2], axis=1)
    fourth = np.block([[c1.T, s1.T], [-s1.T, c1.T]])
    h, l = split_np(first)
    first3 = np.concatenate([h, h, l], axis=1)
    h, l = split_np(second)
    second3 = np.concatenate([h, h, l], axis=0)
    h, l = split_np(third)
    third3 = np.concatenate([h, h, l], axis=0)
    h, l = split_np(fourth)
    fourth3 = np.concatenate([h, h, l], axis=1)
    twiddle = np.stack([np.cos(angt), np.sin(angt)]).astype(np.float32)
    return first3, second3, third3, fourth3, twiddle


def split2(value):
    high = value.astype(bf16)
    low = (value - high.astype(f32)).astype(bf16)
    return high, low


def mm(a, b):
    return jnp.dot(a, b, preferred_element_type=f32)


def mm_pieces(a, b):
    total = None
    for first in range(0, a.shape[1], LANES):
        part = mm(a[:, first : first + LANES], b[first : first + LANES])
        total = part if total is None else total + part
    return total


def band_kernel(
    place_ref, spec_ref, order_ref, weight_ref, first_ref, second_ref, third_ref, fourth_ref, twid_ref,
    out_ref, high_ref, low_ref, line_ref, *, order_count, copies,
):
    blocks, rows, width = spec_ref.shape
    cycles = rows // 6
    n2 = LANES
    k1 = order_count // n2
    n1 = twid_ref.shape[1]
    orders = order_ref[...]
    mask1 = lax.broadcasted_iota(jnp.int32, (k1, order_count), 0) == orders // n2
    mask1 = jnp.where(mask1, 1.0, 0.0).astype(bf16)
    hot2 = lax.broadcasted_iota(jnp.int32, (n2, order_count), 0) == orders % n2
    hot2 = jnp.where(hot2, 1.0, 0.0).astype(bf16)
    for block in range(blocks):
        lanes = slice(block * width, (block + 1) * width)
        value = spec_ref[block]
        low = value - value.astype(bf16).astype(f32)
        line_ref[...] = low
        for row in range(rows):
            span = slice(row * k1, (row + 1) * k1)
            high_ref[span, lanes] = (
                jnp.broadcast_to(spec_ref[block, row : row + 1, :], (k1, width)).astype(bf16) * mask1[:, lanes]
            )
            low_ref[span, lanes] = (
                jnp.broadcast_to(line_ref[row : row + 1, :], (k1, width)).astype(bf16) * mask1[:, lanes]
            )
    contract = (((1,), (1,)), ((), ()))
    ordered = lax.dot_general(high_ref[...], hot2, contract, preferred_element_type=f32)
    ordered = ordered + lax.dot_general(low_ref[...], hot2, contract, preferred_element_type=f32)
    cosine = twid_ref[0]
    sine = twid_ref[1]
    scale = 1.0 / math.sqrt(order_count)
    columns = []
    for cycle in range(cycles):
        for field in range(3):
            first_row = (2 * field * cycles + cycle) * k1
            second_row = first_row + cycles * k1
            columns.append(
                jnp.concatenate(
                    [ordered[first_row : first_row + k1, :], ordered[second_row : second_row + k1, :]], axis=0
                )
            )
    high, low = split2(jnp.concatenate(columns, axis=1))
    part = mm(first_ref[...], jnp.concatenate([high, low, high], axis=0))
    turned = []
    for column in range(3 * cycles):
        lanes = slice(column * n2, (column + 1) * n2)
        re, im = part[:n1, lanes], part[n1:, lanes]
        turned.append(jnp.concatenate([re * cosine - im * sine, re * sine + im * cosine], axis=1))
    high, low = split2(jnp.concatenate(turned, axis=0))
    maps = mm(jnp.concatenate([high, low, high], axis=1), second_ref[...]) * scale
    products = []
    for cycle in range(cycles):
        start = 3 * cycle * n1
        product = maps[start : start + n1] * maps[start + n1 : start + 2 * n1]
        products.append(product * maps[start + 2 * n1 : start + 3 * n1])
    high, low = split2(jnp.concatenate(products, axis=0))
    part = mm(jnp.concatenate([high, low, high], axis=1), third_ref[...])
    turned = []
    for cycle in range(cycles):
        re, im = part[cycle * n1 : (cycle + 1) * n1, :n2], part[cycle * n1 : (cycle + 1) * n1, n2:]
        turned.append(jnp.concatenate([re * cosine + im * sine, im * cosine - re * sine], axis=0))
    high, low = split2(jnp.concatenate(turned, axis=1))
    sums = mm(fourth_ref[...], jnp.concatenate([high, low, high], axis=0))
    factor = NPHI / (n1 * n2) / math.sqrt(NPHI)
    results = [
        sums[:, cycle * n2 : (cycle + 1) * n2] * (weight_ref[0, cycle] * factor) for cycle in range(cycles)
    ]
    high, low = split2(jnp.concatenate(results, axis=0))
    own = order_ref[:, pl.ds(place_ref[0] * width, width)]
    own1 = lax.broadcasted_iota(jnp.int32, (k1, width), 0) == own // n2
    own2 = lax.broadcasted_iota(jnp.int32, (n2, width), 0) == own % n2
    own2 = jnp.where(own2, 1.0, 0.0).astype(bf16)
    picked = mm(jnp.concatenate([high, low], axis=1), jnp.concatenate([own2, own2], axis=0))
    parts = []
    for part in range(2):
        for cycle in range(cycles):
            row = (2 * cycle + part) * k1
            chosen = jnp.where(own1, picked[row : row + k1, :], 0.0)
            parts.append(jnp.sum(chosen, axis=0, keepdims=True))
    weighted = jnp.concatenate(parts, axis=0).astype(bf16)
    for copy in range(copies):
        out_ref[copy] = weighted


def band_step(place, spectra, orders, weights, copies):
    order_count = orders.shape[0]
    tables = fourier_tables(order_count)
    blocks, rows, width = spectra.shape
    k1 = order_count // LANES
    smem = pl.BlockSpec(memory_space=pltpu.SMEM)
    vmem = pl.BlockSpec(memory_space=pltpu.VMEM)
    return pl.pallas_call(
        lambda *refs: band_kernel(*refs, order_count=order_count, copies=copies),
        out_shape=pltpu.VMEM((copies, rows // 3, width), bf16),
        in_specs=[smem, vmem, vmem, smem] + [vmem] * 5,
        out_specs=vmem,
        scratch_shapes=[pltpu.VMEM((rows * k1, order_count), bf16)] * 2 + [pltpu.VMEM((rows, width), f32)],
        compiler_params=pltpu.CompilerParams(vmem_limit_bytes=12 * 2**20),
        name="band",
    )(place, spectra, orders[None, :], weights[None, :], *tables)


CHUNK = 32
GROUP = 16
PAIR = 4
STEP = 32
AHEAD = 3


def synthesis_kernel(alm_ref, leg_ref, out_ref, keep_ref, alm_buf, acc_ref, row_ref, alm_sem, leg_sem, *, bands):
    fields, m_dev, l_dev = alm_ref.shape
    cycle_count = leg_ref.shape[1]
    cycles = cycle_count // bands
    chunks = m_dev // STEP
    per_tile = LANES // GROUP

    def alm_copy(chunk):
        rows = pl.ds(chunk * STEP, STEP)
        return pltpu.make_async_copy(alm_ref.at[:, rows], alm_buf.at[:, rows], alm_sem.at[chunk])

    def leg_copy(chunk):
        rows = pl.ds(chunk * STEP, STEP)
        return pltpu.make_async_copy(leg_ref.at[rows], keep_ref.at[rows], leg_sem.at[chunk])

    for chunk in range(min(AHEAD, chunks)):
        alm_copy(chunk).start()
        leg_copy(chunk).start()
    width = fields * GROUP
    lane = lax.broadcasted_iota(jnp.int32, (1, width), 1) % GROUP
    tile_lane = lax.broadcasted_iota(jnp.int32, (1, LANES), 1) // GROUP

    def one_tile(tile, carry):
        sums = [None] * fields
        for place in range(per_tile):
            number = tile * per_tile + place
            if place * GROUP % STEP == 0:
                chunk = number * GROUP // STEP

                @pl.when(chunk + AHEAD < chunks)
                def _():
                    alm_copy(chunk + AHEAD).start()
                    leg_copy(chunk + AHEAD).start()

                alm_copy(chunk).wait()
                leg_copy(chunk).wait()
            rows = pl.ds(number * GROUP, GROUP)
            right = alm_buf[:, rows, :].reshape(width, l_dev)
            own = None
            for half in range(2):
                left = keep_ref[pl.ds(number * GROUP + half * GROUP // 2, GROUP // 2)]
                both = lax.dot_general(
                    left.reshape(GROUP // 2 * cycle_count, l_dev),
                    right,
                    (((1,), (1,)), ((), ())),
                    preferred_element_type=f32,
                )
                for order in range(GROUP // 2):
                    part = both[order * cycle_count : (order + 1) * cycle_count]
                    part = jnp.where(lane == half * GROUP // 2 + order, part, 0.0)
                    own = part if own is None else own + part
            own = jnp.concatenate([own, jnp.zeros((cycle_count, LANES - width), f32)], axis=1)
            for field in range(fields):
                shift = (place - field) * GROUP % LANES
                moved = pltpu.roll(own, shift, 1) if shift else own
                moved = jnp.where(tile_lane == place, moved, 0.0)
                sums[field] = moved if sums[field] is None else sums[field] + moved
        for field in range(fields):
            acc_ref[tile, field] = sums[field]
        return carry

    lax.fori_loop(0, m_dev // LANES, one_tile, 0)
    for tile in range(m_dev // LANES):
        lanes = slice(tile * LANES, (tile + 1) * LANES)
        for band in range(bands):
            for field in range(fields):
                row_ref[band, field * cycles : (field + 1) * cycles, lanes] = acc_ref[
                    tile, field, band * cycles : (band + 1) * cycles, :
                ]
    out_ref[...] = row_ref[...].astype(bf16)


def synthesis(coeffs, legendre, bands):
    fields, m_dev, l_dev = coeffs.shape
    cycle_count = legendre.shape[1]
    rows = fields * cycle_count // bands
    chunks = m_dev // STEP
    hbm = pl.BlockSpec(memory_space=pl.ANY)
    vmem = pl.BlockSpec(memory_space=pltpu.VMEM)
    return pl.pallas_call(
        lambda *refs: synthesis_kernel(*refs, bands=bands),
        out_shape=[
            jax.ShapeDtypeStruct((bands, rows, m_dev), bf16),
            pltpu.VMEM(legendre.shape, bf16),
        ],
        in_specs=[hbm, hbm],
        out_specs=[vmem, vmem],
        scratch_shapes=[
            pltpu.VMEM(coeffs.shape, bf16),
            pltpu.VMEM((m_dev // LANES, fields, cycle_count, LANES), f32),
            pltpu.VMEM((bands, rows, m_dev), f32),
            pltpu.SemaphoreType.DMA((chunks,)),
            pltpu.SemaphoreType.DMA((chunks,)),
        ],
        compiler_params=pltpu.CompilerParams(vmem_limit_bytes=11 * 2**20),
        name="synthesis",
    )(
        pltpu.with_memory_space_constraint(coeffs, pltpu.HBM),
        pltpu.with_memory_space_constraint(legendre, pltpu.HBM),
    )


def analysis_kernel(weighted_ref, keep_ref, out_ref, rows_ref, wide_ref, left_ref, buf_ref, sem, *, scale):
    bands, part_rows, m_dev = weighted_ref.shape
    cycles = part_rows // 2
    cycle_count, l_dev = keep_ref.shape[1:]
    width = CHUNK * cycle_count
    pair = left_ref.shape[1]
    chunks = m_dev // CHUNK
    steps = chunks // pair
    spread = lax.broadcasted_iota(jnp.int32, (cycle_count, width), 1) % cycle_count
    spread = spread == lax.broadcasted_iota(jnp.int32, (cycle_count, width), 0)
    spread = jnp.where(spread, 1.0, 0.0).astype(bf16)
    for part in range(2):
        for band in range(bands):
            rows_ref[part, band * cycles : (band + 1) * cycles, :] = weighted_ref[
                band, part * cycles : (part + 1) * cycles, :
            ].astype(f32)
        wide_ref[:, part] = rows_ref[part].T.astype(bf16).reshape(chunks, CHUNK, cycle_count)
    diagonal = lax.broadcasted_iota(jnp.int32, (CHUNK, width), 1) // cycle_count
    diagonal = diagonal == lax.broadcasted_iota(jnp.int32, (CHUNK, width), 0)

    def build(step, slot):
        source = wide_ref[pl.ds(step * pair, pair)].reshape(pair * 2 * CHUNK, cycle_count)
        tiled = mm(source, spread).reshape(pair, 2, CHUNK, width)
        chosen = jnp.where(diagonal, tiled, 0.0).astype(bf16)
        left_ref[slot] = chosen.reshape(pair, 2 * CHUNK, width)

    def out_copy(step, slot):
        rows = pl.ds(step * pair * CHUNK, pair * CHUNK)
        return pltpu.make_async_copy(buf_ref.at[slot], out_ref.at[:, rows], sem.at[slot])

    build(0, 0)

    def one_step(step, carry):
        slot = step % 2

        @pl.when(step >= 2)
        def _():
            out_copy(step - 2, slot).wait()

        for item in range(pair):
            rows = pl.ds((step * pair + item) * CHUNK, CHUNK)
            right = keep_ref[rows].reshape(width, l_dev)
            result = mm_pieces(left_ref[slot, item], right) * scale
            buf_ref[slot, :, item * CHUNK : (item + 1) * CHUNK, :] = result.reshape(2, CHUNK, l_dev).astype(bf16)
        build(jnp.minimum(step + 1, steps - 1), 1 - slot)
        out_copy(step, slot).start()
        return carry

    lax.fori_loop(0, steps, one_step, 0)
    for step in range(max(steps - 2, 0), steps):
        out_copy(step, step % 2).wait()


def analysis(weighted, keep, scale):
    m_dev, cycle_count, l_dev = keep.shape
    vmem = pl.BlockSpec(memory_space=pltpu.VMEM)
    chunks = m_dev // CHUNK
    pair = math.gcd(chunks, PAIR)
    return pl.pallas_call(
        lambda *refs: analysis_kernel(*refs, scale=scale),
        out_shape=jax.ShapeDtypeStruct((2, m_dev, l_dev), bf16),
        in_specs=[vmem, vmem],
        out_specs=pl.BlockSpec(memory_space=pl.ANY),
        scratch_shapes=[
            pltpu.VMEM((2, cycle_count, m_dev), f32),
            pltpu.VMEM((chunks, 2, CHUNK, cycle_count), bf16),
            pltpu.VMEM((2, pair, 2 * CHUNK, CHUNK * cycle_count), bf16),
            pltpu.VMEM((2, 2, pair * CHUNK, l_dev), bf16),
            pltpu.SemaphoreType.DMA((2,)),
        ],
        compiler_params=pltpu.CompilerParams(vmem_limit_bytes=14 * 2**20),
        name="analysis",
    )(
        pltpu.with_memory_space_constraint(weighted, pltpu.VMEM),
        pltpu.with_memory_space_constraint(keep, pltpu.VMEM),
    )


def shards(alm, legendre, m_value, cycle_weight):
    m_dev, cycle_count, l_dev = legendre.shape
    bands = lax.axis_size("blk")
    place = lax.axis_index("mblk").astype(jnp.int32)[None]
    outgoing, keep = synthesis(alm.reshape(6, m_dev, l_dev), legendre, bands)
    outgoing, place, cycle_weight = lax.optimization_barrier((outgoing, place, cycle_weight))
    incoming = lax.all_to_all(outgoing, "blk", 0, 0, tiled=True)
    spectra = jnp.sum(incoming.astype(f32), axis=0)
    gathered = lax.all_gather(spectra, "mblk", axis=0)
    copies = band_step(place, gathered, m_value, cycle_weight, bands)
    weighted = lax.all_to_all(copies, "blk", 0, 0, tiled=True)
    return analysis(weighted, keep, math.sqrt(l_dev * bands / cycle_count))


def solution(mesh):
    in_specs = (P(None, None, "mblk", "blk"), P("mblk", None, "blk"), P(), P("blk"))
    out_specs = P(None, "mblk", "blk")
    return jax.shard_map(shards, mesh=mesh, in_specs=in_specs, out_specs=out_specs, check_vma=False)
```

```python
import math

import jax
import jax.numpy as jnp
import numpy as np
from jax import lax
from jax.experimental import pallas as pl
from jax.experimental.pallas import tpu as pltpu
from jax.sharding import PartitionSpec as P

NPHI = 32768
LANES = 128

f32 = jnp.float32
bf16 = jnp.bfloat16


def grid_size(order_count):
    size = LANES
    while size <= 4 * (order_count - 1):
        size *= 2
    return min(size, NPHI)


def split_np(table):
    high = table.astype(jnp.bfloat16)
    low = (table - high.astype(np.float64)).astype(jnp.bfloat16)
    return high, low


def fourier_tables(order_count):
    size = grid_size(order_count)
    n2 = LANES
    n1 = size // n2
    k1 = order_count // n2
    turn = 2.0 * np.pi
    ang1 = turn * (np.outer(np.arange(n1), np.arange(k1)) % n1) / n1
    c1, s1 = np.cos(ang1), np.sin(ang1)
    ang2 = turn * (np.outer(np.arange(n2), np.arange(n2)) % n2) / n2
    c2, s2 = np.cos(ang2), np.sin(ang2)
    angt = turn * np.outer(np.arange(n1), np.arange(n2)) / size
    first = np.block([[c1, -s1], [s1, c1]])
    second = np.concatenate([c2, -s2], axis=0)
    third = np.concatenate([c2, -s2], axis=1)
    fourth = np.block([[c1.T, s1.T], [-s1.T, c1.T]])
    h, l = split_np(first)
    first3 = np.concatenate([h, h, l], axis=1)
    h, l = split_np(second)
    second3 = np.concatenate([h, h, l], axis=0)
    h, l = split_np(third)
    third3 = np.concatenate([h, h, l], axis=0)
    h, l = split_np(fourth)
    fourth3 = np.concatenate([h, h, l], axis=1)
    twiddle = np.stack([np.cos(angt), np.sin(angt)]).astype(np.float32)
    return first3, second3, third3, fourth3, twiddle


def split2(value):
    high = value.astype(bf16)
    low = (value - high.astype(f32)).astype(bf16)
    return high, low


def mm(a, b):
    return jnp.dot(a, b, preferred_element_type=f32)


def mm_pieces(a, b):
    total = None
    for first in range(0, a.shape[1], LANES):
        part = mm(a[:, first : first + LANES], b[first : first + LANES])
        total = part if total is None else total + part
    return total


def band_kernel(
    place_ref, spec_ref, order_ref, weight_ref, first_ref, second_ref, third_ref, fourth_ref, twid_ref,
    out_ref, high_ref, low_ref, line_ref, *, order_count, copies,
):
    blocks, rows, width = spec_ref.shape
    cycles = rows // 6
    n2 = LANES
    k1 = order_count // n2
    n1 = twid_ref.shape[1]
    orders = order_ref[...]
    mask1 = lax.broadcasted_iota(jnp.int32, (k1, order_count), 0) == orders // n2
    mask1 = jnp.where(mask1, 1.0, 0.0).astype(bf16)
    hot2 = lax.broadcasted_iota(jnp.int32, (n2, order_count), 0) == orders % n2
    hot2 = jnp.where(hot2, 1.0, 0.0).astype(bf16)
    for block in range(blocks):
        lanes = slice(block * width, (block + 1) * width)
        value = spec_ref[block]
        low = value - value.astype(bf16).astype(f32)
        line_ref[...] = low
        for row in range(rows):
            span = slice(row * k1, (row + 1) * k1)
            high_ref[span, lanes] = (
                jnp.broadcast_to(spec_ref[block, row : row + 1, :], (k1, width)).astype(bf16) * mask1[:, lanes]
            )
            low_ref[span, lanes] = (
                jnp.broadcast_to(line_ref[row : row + 1, :], (k1, width)).astype(bf16) * mask1[:, lanes]
            )
    contract = (((1,), (1,)), ((), ()))
    ordered = lax.dot_general(high_ref[...], hot2, contract, preferred_element_type=f32)
    ordered = ordered + lax.dot_general(low_ref[...], hot2, contract, preferred_element_type=f32)
    cosine = twid_ref[0]
    sine = twid_ref[1]
    scale = 1.0 / math.sqrt(order_count)
    columns = []
    for cycle in range(cycles):
        for field in range(3):
            first_row = (2 * field * cycles + cycle) * k1
            second_row = first_row + cycles * k1
            columns.append(
                jnp.concatenate(
                    [ordered[first_row : first_row + k1, :], ordered[second_row : second_row + k1, :]], axis=0
                )
            )
    high, low = split2(jnp.concatenate(columns, axis=1))
    part = mm(first_ref[...], jnp.concatenate([high, low, high], axis=0))
    turned = []
    for column in range(3 * cycles):
        lanes = slice(column * n2, (column + 1) * n2)
        re, im = part[:n1, lanes], part[n1:, lanes]
        turned.append(jnp.concatenate([re * cosine - im * sine, re * sine + im * cosine], axis=1))
    high, low = split2(jnp.concatenate(turned, axis=0))
    maps = mm(jnp.concatenate([high, low, high], axis=1), second_ref[...]) * scale
    products = []
    for cycle in range(cycles):
        start = 3 * cycle * n1
        product = maps[start : start + n1] * maps[start + n1 : start + 2 * n1]
        products.append(product * maps[start + 2 * n1 : start + 3 * n1])
    high, low = split2(jnp.concatenate(products, axis=0))
    part = mm(jnp.concatenate([high, low, high], axis=1), third_ref[...])
    turned = []
    for cycle in range(cycles):
        re, im = part[cycle * n1 : (cycle + 1) * n1, :n2], part[cycle * n1 : (cycle + 1) * n1, n2:]
        turned.append(jnp.concatenate([re * cosine + im * sine, im * cosine - re * sine], axis=0))
    high, low = split2(jnp.concatenate(turned, axis=1))
    sums = mm(fourth_ref[...], jnp.concatenate([high, low, high], axis=0))
    factor = NPHI / (n1 * n2) / math.sqrt(NPHI)
    results = [
        sums[:, cycle * n2 : (cycle + 1) * n2] * (weight_ref[0, cycle] * factor) for cycle in range(cycles)
    ]
    high, low = split2(jnp.concatenate(results, axis=0))
    own = order_ref[:, pl.ds(place_ref[0] * width, width)]
    own1 = lax.broadcasted_iota(jnp.int32, (k1, width), 0) == own // n2
    own2 = lax.broadcasted_iota(jnp.int32, (n2, width), 0) == own % n2
    own2 = jnp.where(own2, 1.0, 0.0).astype(bf16)
    picked = mm(jnp.concatenate([high, low], axis=1), jnp.concatenate([own2, own2], axis=0))
    parts = []
    for part in range(2):
        for cycle in range(cycles):
            row = (2 * cycle + part) * k1
            chosen = jnp.where(own1, picked[row : row + k1, :], 0.0)
            parts.append(jnp.sum(chosen, axis=0, keepdims=True))
    weighted = jnp.concatenate(parts, axis=0).astype(bf16)
    for copy in range(copies):
        out_ref[copy] = weighted


def band_step(place, spectra, orders, weights, copies):
    order_count = orders.shape[0]
    tables = fourier_tables(order_count)
    blocks, rows, width = spectra.shape
    k1 = order_count // LANES
    smem = pl.BlockSpec(memory_space=pltpu.SMEM)
    vmem = pl.BlockSpec(memory_space=pltpu.VMEM)
    return pl.pallas_call(
        lambda *refs: band_kernel(*refs, order_count=order_count, copies=copies),
        out_shape=pltpu.VMEM((copies, rows // 3, width), bf16),
        in_specs=[smem, vmem, vmem, smem] + [vmem] * 5,
        out_specs=vmem,
        scratch_shapes=[pltpu.VMEM((rows * k1, order_count), bf16)] * 2 + [pltpu.VMEM((rows, width), f32)],
        compiler_params=pltpu.CompilerParams(vmem_limit_bytes=12 * 2**20),
        name="band",
    )(place, spectra, orders[None, :], weights[None, :], *tables)


CHUNK = 32
GROUP = 16
PAIR = 4
STEP = 32
AHEAD = 5


def synthesis_kernel(alm_ref, leg_ref, out_ref, keep_ref, alm_buf, acc_ref, row_ref, alm_sem, leg_sem, *, bands):
    fields, m_dev, l_dev = alm_ref.shape
    cycle_count = leg_ref.shape[1]
    cycles = cycle_count // bands
    chunks = m_dev // STEP
    per_tile = LANES // GROUP

    def alm_copy(chunk):
        rows = pl.ds(chunk * STEP, STEP)
        return pltpu.make_async_copy(alm_ref.at[:, rows], alm_buf.at[:, rows], alm_sem.at[chunk])

    def leg_copy(chunk):
        rows = pl.ds(chunk * STEP, STEP)
        return pltpu.make_async_copy(leg_ref.at[rows], keep_ref.at[rows], leg_sem.at[chunk])

    for chunk in range(min(AHEAD, chunks)):
        alm_copy(chunk).start()
        leg_copy(chunk).start()
    width = fields * GROUP
    lane = lax.broadcasted_iota(jnp.int32, (1, width), 1) % GROUP
    tile_lane = lax.broadcasted_iota(jnp.int32, (1, LANES), 1) // GROUP

    def one_tile(tile, carry):
        sums = [None] * fields
        for place in range(per_tile):
            number = tile * per_tile + place
            if place * GROUP % STEP == 0:
                chunk = number * GROUP // STEP

                @pl.when(chunk + AHEAD < chunks)
                def _():
                    alm_copy(chunk + AHEAD).start()
                    leg_copy(chunk + AHEAD).start()

                alm_copy(chunk).wait()
                leg_copy(chunk).wait()
            rows = pl.ds(number * GROUP, GROUP)
            right = alm_buf[:, rows, :].reshape(width, l_dev)
            own = None
            for half in range(2):
                left = keep_ref[pl.ds(number * GROUP + half * GROUP // 2, GROUP // 2)]
                both = lax.dot_general(
                    left.reshape(GROUP // 2 * cycle_count, l_dev),
                    right,
                    (((1,), (1,)), ((), ())),
                    preferred_element_type=f32,
                )
                for order in range(GROUP // 2):
                    part = both[order * cycle_count : (order + 1) * cycle_count]
                    part = jnp.where(lane == half * GROUP // 2 + order, part, 0.0)
                    own = part if own is None else own + part
            own = jnp.concatenate([own, jnp.zeros((cycle_count, LANES - width), f32)], axis=1)
            for field in range(fields):
                shift = (place - field) * GROUP % LANES
                moved = pltpu.roll(own, shift, 1) if shift else own
                moved = jnp.where(tile_lane == place, moved, 0.0)
                sums[field] = moved if sums[field] is None else sums[field] + moved
        for field in range(fields):
            acc_ref[tile, field] = sums[field]
        return carry

    lax.fori_loop(0, m_dev // LANES, one_tile, 0)
    for tile in range(m_dev // LANES):
        lanes = slice(tile * LANES, (tile + 1) * LANES)
        for band in range(bands):
            for field in range(fields):
                row_ref[band, field * cycles : (field + 1) * cycles, lanes] = acc_ref[
                    tile, field, band * cycles : (band + 1) * cycles, :
                ]
    out_ref[...] = row_ref[...].astype(bf16)


def synthesis(coeffs, legendre, bands):
    fields, m_dev, l_dev = coeffs.shape
    cycle_count = legendre.shape[1]
    rows = fields * cycle_count // bands
    chunks = m_dev // STEP
    hbm = pl.BlockSpec(memory_space=pl.ANY)
    vmem = pl.BlockSpec(memory_space=pltpu.VMEM)
    return pl.pallas_call(
        lambda *refs: synthesis_kernel(*refs, bands=bands),
        out_shape=[
            jax.ShapeDtypeStruct((bands, rows, m_dev), bf16),
            pltpu.VMEM(legendre.shape, bf16),
        ],
        in_specs=[hbm, hbm],
        out_specs=[vmem, vmem],
        scratch_shapes=[
            pltpu.VMEM(coeffs.shape, bf16),
            pltpu.VMEM((m_dev // LANES, fields, cycle_count, LANES), f32),
            pltpu.VMEM((bands, rows, m_dev), f32),
            pltpu.SemaphoreType.DMA((chunks,)),
            pltpu.SemaphoreType.DMA((chunks,)),
        ],
        compiler_params=pltpu.CompilerParams(vmem_limit_bytes=11 * 2**20),
        name="synthesis",
    )(
        pltpu.with_memory_space_constraint(coeffs, pltpu.HBM),
        pltpu.with_memory_space_constraint(legendre, pltpu.HBM),
    )


def analysis_kernel(weighted_ref, keep_ref, out_ref, rows_ref, wide_ref, left_ref, buf_ref, sem, *, scale):
    bands, part_rows, m_dev = weighted_ref.shape
    cycles = part_rows // 2
    cycle_count, l_dev = keep_ref.shape[1:]
    width = CHUNK * cycle_count
    pair = left_ref.shape[1]
    chunks = m_dev // CHUNK
    steps = chunks // pair
    spread = lax.broadcasted_iota(jnp.int32, (cycle_count, width), 1) % cycle_count
    spread = spread == lax.broadcasted_iota(jnp.int32, (cycle_count, width), 0)
    spread = jnp.where(spread, 1.0, 0.0).astype(bf16)
    for part in range(2):
        for band in range(bands):
            rows_ref[part, band * cycles : (band + 1) * cycles, :] = weighted_ref[
                band, part * cycles : (part + 1) * cycles, :
            ].astype(f32)
        wide_ref[:, part] = rows_ref[part].T.astype(bf16).reshape(chunks, CHUNK, cycle_count)
    diagonal = lax.broadcasted_iota(jnp.int32, (CHUNK, width), 1) // cycle_count
    diagonal = diagonal == lax.broadcasted_iota(jnp.int32, (CHUNK, width), 0)

    def build(step, slot):
        source = wide_ref[pl.ds(step * pair, pair)].reshape(pair * 2 * CHUNK, cycle_count)
        tiled = mm(source, spread).reshape(pair, 2, CHUNK, width)
        chosen = jnp.where(diagonal, tiled, 0.0).astype(bf16)
        left_ref[slot] = chosen.reshape(pair, 2 * CHUNK, width)

    def out_copy(step, slot, item):
        rows = pl.ds((step * pair + item) * CHUNK, CHUNK)
        return pltpu.make_async_copy(buf_ref.at[slot, item], out_ref.at[:, rows], sem.at[slot, item])

    build(0, 0)

    def one_step(step, carry):
        slot = step % 2

        @pl.when(step >= 2)
        def _():
            for item in range(pair):
                out_copy(step - 2, slot, item).wait()

        build(jnp.minimum(step + 1, steps - 1), 1 - slot)
        for item in range(pair):
            rows = pl.ds((step * pair + item) * CHUNK, CHUNK)
            right = keep_ref[rows].reshape(width, l_dev)
            result = mm_pieces(left_ref[slot, item], right) * scale
            buf_ref[slot, item] = result.reshape(2, CHUNK, l_dev).astype(bf16)
            out_copy(step, slot, item).start()
        return carry

    lax.fori_loop(0, steps, one_step, 0)
    for step in range(max(steps - 2, 0), steps):
        for item in range(pair):
            out_copy(step, step % 2, item).wait()


def analysis(weighted, keep, scale):
    m_dev, cycle_count, l_dev = keep.shape
    vmem = pl.BlockSpec(memory_space=pltpu.VMEM)
    chunks = m_dev // CHUNK
    pair = math.gcd(chunks, PAIR)
    return pl.pallas_call(
        lambda *refs: analysis_kernel(*refs, scale=scale),
        out_shape=jax.ShapeDtypeStruct((2, m_dev, l_dev), bf16),
        in_specs=[vmem, vmem],
        out_specs=pl.BlockSpec(memory_space=pl.ANY),
        scratch_shapes=[
            pltpu.VMEM((2, cycle_count, m_dev), f32),
            pltpu.VMEM((chunks, 2, CHUNK, cycle_count), bf16),
            pltpu.VMEM((2, pair, 2 * CHUNK, CHUNK * cycle_count), bf16),
            pltpu.VMEM((2, pair, 2, CHUNK, l_dev), bf16),
            pltpu.SemaphoreType.DMA((2, pair)),
        ],
        compiler_params=pltpu.CompilerParams(vmem_limit_bytes=14 * 2**20),
        name="analysis",
    )(
        pltpu.with_memory_space_constraint(weighted, pltpu.VMEM),
        pltpu.with_memory_space_constraint(keep, pltpu.VMEM),
    )


def shards(alm, legendre, m_value, cycle_weight):
    m_dev, cycle_count, l_dev = legendre.shape
    bands = lax.axis_size("blk")
    place = lax.axis_index("mblk").astype(jnp.int32)[None]
    outgoing, keep = synthesis(alm.reshape(6, m_dev, l_dev), legendre, bands)
    outgoing, place, cycle_weight = lax.optimization_barrier((outgoing, place, cycle_weight))
    incoming = lax.all_to_all(outgoing, "blk", 0, 0, tiled=True)
    spectra = jnp.sum(incoming.astype(f32), axis=0)
    gathered = lax.all_gather(spectra, "mblk", axis=0)
    copies = band_step(place, gathered, m_value, cycle_weight, bands)
    weighted = lax.all_to_all(copies, "blk", 0, 0, tiled=True)
    return analysis(weighted, keep, math.sqrt(l_dev * bands / cycle_count))


def solution(mesh):
    in_specs = (P(None, None, "mblk", "blk"), P("mblk", None, "blk"), P(), P("blk"))
    out_specs = P(None, "mblk", "blk")
    return jax.shard_map(shards, mesh=mesh, in_specs=in_specs, out_specs=out_specs, check_vma=False)
```
